32 devices in a mesh: groups: 2 (over x), ctx: 16 (over z, y, core).
Axes of the slice: x: 2, y: 2, z: 4, core: 2. Of those that a mesh axis runs over, the one named last changes fastest.
Arguments:
- keys: bfloat16 [16384, 128], P(('groups', 'ctx')), parts along dimension 0, may hold values from -6 to 6
- queries: bfloat16 [8192, 1024], P(('groups', 'ctx')), parts along dimension 0, may hold values from -240 to 240
- teacher_map: bfloat16 [8192, 512], P(('groups', 'ctx')), parts along dimension 0, may hold values from 0.0099487305 to 1
- slab_index: int32 [32], P(('groups', 'ctx')), parts along dimension 0, may hold values from 0 to 31
- pos_gain: float32 [32, 128], replicated, may hold values from 0.1 to 1.9
- w_comp: bfloat16 [128, 128], replicated, may hold values from -0.09375 to 0.09375
Outputs:
- loss: float32 [2], P('groups'), parts along dimension 0
- grad_queries: bfloat16 [8192, 1024], P(('groups', 'ctx')), parts along dimension 0
- grad_keys: bfloat16 [16384, 128], P(('groups', 'ctx')), parts along dimension 0
- grad_comp: float32 [256, 128], P('groups'), parts along dimension 0
- grad_gain: float32 [64, 128], P('groups'), parts along dimension 0
The draws below stay inside these ranges and needn't reach their ends.
There are 2 independent parts, one for each index of `groups`. The reference program is written for one: setup_inputs(seed, part) draws one part's arguments, and reference() takes and returns one part's arrays. A program takes and returns all parts, laid end to end along the dimension named above; an argument that names none is the same for every part. Nothing has to cross between parts.
All inputs are finite; a program needn't handle non-finite values.
Results may differ from the reference program's by a relative error of at most 0.009.
The reference program's roundings to bfloat16 on the way count: a program that leaves them out, or rounds other values in their place, can miss the bound.
Values may be sent and summed in bfloat16 or wider, within the bound.
A program may use at most 64 MiB of HBM per device.

```python
import math
import jax
import jax.numpy as jnp
from jax import lax

DH = 128
HEADS = 8
KERNEL = 32
STRIDE = 16
QDEV = 256
SEQ = 8192
NBLK = 512
NQ = 4096
N_CTX = 16


def draw_queries(key, part):
    first = jax.random.fold_in(key, 11)
    values = jax.random.truncated_normal(first, -6.0, 6.0, (NQ, HEADS * DH), jnp.float32)
    return values.astype(jnp.bfloat16)


def place_ends(entries, stream_key, low, high):
    shape = entries.shape
    index_at = [jax.random.randint(jax.random.fold_in(stream_key, axis), (), 0, shape[axis]) for axis in range(len(shape))]
    entries = entries.at[tuple(index_at)].set(low)
    longest = shape.index(max(shape))
    index_at[longest] = (index_at[longest] + 1) % shape[longest]
    return entries.at[tuple(index_at)].set(high)


def levels(stream_key, shape, cuts, low, top_value):
    gain = 1.0
    for position, parts in cuts:
        steps = jax.random.uniform(jax.random.fold_in(jax.random.fold_in(stream_key, 6), position), (parts,), jnp.float32, low / len(cuts), top_value / len(cuts))
        gain = gain * jnp.repeat(jnp.exp(steps), shape[position] // parts).reshape((-1,) + (1,) * (len(shape) - 1 - position))
    return gain


def normal_values(own_key, extent, deviation, most, pieces=(), kind=jnp.bfloat16):
    result = jax.random.normal(own_key, extent, jnp.float32) * deviation
    if len(pieces) > 0:
        result = levels(own_key, extent, pieces, -0.22, 0.18) * result
    return jnp.clip(result, min=-most, max=most).astype(kind)


def setup_inputs(seed: int = 0, part: int = 0) -> dict:
    splits = jax.random.split(jax.random.key(seed), 7)
    part_splits = jax.random.split(jax.random.fold_in(splits[6], part), 7)
    return {
        "keys": normal_values(part_splits[0], (SEQ, DH), 1.0, 6.0, ((0, 16),)),
        "queries": draw_queries(jax.random.fold_in(jax.random.fold_in(splits[6], part), 71), part),
        "teacher_map": jnp.clip(jnp.exp(math.log(1.0) - 4.61031033 * jax.random.uniform(part_splits[2], (NQ, NBLK), jnp.float32) ** levels(part_splits[2], (NQ, NBLK), ((0, 16),), -0.2, 0.2)), 0.0099487305, 1.0).astype(jnp.bfloat16),
        "slab_index": place_ends(jax.random.randint(part_splits[3], (N_CTX,), 0, SEQ // QDEV), jax.random.fold_in(part_splits[3], 1), 0, (SEQ // QDEV) - 1).astype(jnp.int32),
        "pos_gain": jnp.clip(1.0 + 0.18 * jax.random.normal(splits[4], (KERNEL, DH), jnp.float32), 0.1, 1.9),
        "w_comp": normal_values(splits[5], (DH, DH), (KERNEL * DH) ** -0.5, 0.09375),
    }


big_negative = -1.0e30
loss_scale = 256.0


def pool_keys(keys, pos_gain):
    padded = jnp.concatenate([keys, jnp.zeros((STRIDE, DH), keys.dtype)], axis=0)
    lower = padded[:SEQ].reshape(NBLK, STRIDE, DH).astype(jnp.float32)
    upper = padded[STRIDE:].reshape(NBLK, STRIDE, DH).astype(jnp.float32)
    pooled = jnp.sum(lower * pos_gain[:STRIDE], axis=1) + jnp.sum(upper * pos_gain[STRIDE:], axis=1)
    return lower, upper, pooled.astype(jnp.bfloat16)


def slab_terms(query_rows, teacher_rows, places, comp):
    inv = DH ** -0.5
    count = query_rows.shape[0]
    heads_f = query_rows.reshape(count, HEADS, DH).astype(jnp.float32)
    comp_f = comp.astype(jnp.float32)
    scores = jnp.einsum("thd,jd->htj", heads_f, comp_f) * inv
    column = jnp.arange(NBLK, dtype=jnp.int32)
    visible = (STRIDE * column + KERNEL - 1)[None, :] <= places[:, None]
    masked = jnp.where(visible[None], scores, big_negative)
    top = jnp.max(masked, axis=2, keepdims=True)
    expo = jnp.where(visible[None], jnp.exp(masked - top), 0.0)
    total = jnp.sum(expo, axis=2, keepdims=True)
    lse = jnp.where(total > 0, top + jnp.log(jnp.where(total > 0, total, 1.0)), 0.0)
    shifted = jnp.where(visible[None], scores - lse, big_negative)
    head_top = jnp.max(shifted, axis=0)
    logm = head_top + jnp.log(jnp.sum(jnp.exp(shifted - head_top), axis=0)) - jnp.log(jnp.float32(HEADS))
    logm = jnp.where(visible, logm, 0.0)
    prob = jnp.where(visible[None], jnp.exp(shifted), 0.0)
    ratio = jnp.where(visible[None], jnp.exp(shifted - logm[None]), 0.0) / HEADS
    teach = teacher_rows.astype(jnp.float32)
    teach_total = jnp.sum(jnp.where(visible, teach, 0.0), axis=1, keepdims=True)
    safe_total = jnp.where(teach_total > 0, teach_total, 1.0)
    tprob = jnp.where(visible, teach / safe_total, 0.0)
    logt = jnp.where(visible, jnp.log(teach) - jnp.log(safe_total), 0.0)
    kl_sum = jnp.sum(tprob * (logt - logm))
    cvec = jnp.sum(tprob[None] * ratio, axis=2)
    grad = (loss_scale * (prob * cvec[..., None] - tprob[None] * ratio)).astype(jnp.bfloat16)
    grad_f = grad.astype(jnp.float32)
    grad_q = jnp.einsum("htj,jd->thd", grad_f, comp_f) * inv
    grad_c = jnp.einsum("htj,thd->jd", grad_f, heads_f) * inv
    return kl_sum, grad_q.reshape(count, HEADS * DH).astype(jnp.bfloat16), grad_c


def reference(keys, queries, teacher_map, slab_index, pos_gain, w_comp):
    lower, upper, pooled = pool_keys(keys, pos_gain)
    comp = jnp.dot(pooled, w_comp, preferred_element_type=jnp.float32).astype(jnp.bfloat16)
    places = slab_index[:, None] * QDEV + jnp.arange(QDEV, dtype=jnp.int32)[None, :]

    def step(carry, items):
        q_rows, t_rows, p_rows = items
        kl_sum, grad_q, grad_c = slab_terms(q_rows, t_rows, p_rows, comp)
        return (carry[0] + kl_sum, carry[1] + grad_c), grad_q

    start = (jnp.zeros((), jnp.float32), jnp.zeros((NBLK, DH), jnp.float32))
    items = (queries.reshape(N_CTX, QDEV, HEADS * DH), teacher_map.reshape(N_CTX, QDEV, NBLK), places)
    (kl_total, grad_comp_keys), grad_rows = lax.scan(step, start, items)
    loss = (kl_total / NQ).reshape(1)
    grad_queries = grad_rows.reshape(NQ, HEADS * DH)
    highest = lax.Precision.HIGHEST
    grad_pooled = jnp.dot(grad_comp_keys, w_comp.astype(jnp.float32).T, precision=highest)
    grad_comp = jnp.dot(pooled.astype(jnp.float32).T, grad_comp_keys, precision=highest)
    gain_low = jnp.einsum("jd,jpd->pd", grad_pooled, lower, precision=highest)
    gain_high = jnp.einsum("jd,jpd->pd", grad_pooled, upper, precision=highest)
    grad_gain = jnp.concatenate([gain_low, gain_high], axis=0)
    low_part = (grad_pooled[:, None, :] * pos_gain[:STRIDE]).reshape(SEQ, DH)
    high_part = (grad_pooled[:, None, :] * pos_gain[STRIDE:]).reshape(SEQ, DH)
    shifted_high = jnp.concatenate([jnp.zeros((STRIDE, DH), jnp.float32), high_part[:-STRIDE]], axis=0)
    grad_keys = (low_part + shifted_high).astype(jnp.bfloat16)
    return loss, grad_queries, grad_keys, grad_comp, grad_gain
```

```python
import functools

import jax
import jax.numpy as jnp
from jax import lax
from jax.experimental import pallas as pl
from jax.experimental.pallas import tpu as pltpu
from jax.sharding import PartitionSpec as P

DH = 128
HEADS = 8
KERNEL = 32
STRIDE = 16
CHUNK = 512

big_negative = -1e30
loss_scale = 256.0
f32 = jnp.float32
bf16 = jnp.bfloat16


def split3(x):
    first = x.astype(bf16)
    rest = x - first.astype(f32)
    second = rest.astype(bf16)
    third = (rest - second.astype(f32)).astype(bf16)
    return first, second, third


def remote(src, dst, send_sem, recv_sem, device):
    return pltpu.make_async_remote_copy(
        src_ref=src,
        dst_ref=dst,
        send_sem=send_sem,
        recv_sem=recv_sem,
        device_id={"ctx": device},
        device_id_type=pl.DeviceIdType.MESH,
    )


def kernel(
    n, rb, tr, rc, rg,
    slab_ref, keys_ref, gain_ref, w_ref, q_hbm, t_hbm,
    loss_ref, gq_hbm, gk_ref, gcomp_ref, ggain_ref,
    q_v, t_v, gq_v, pool_v, part_v, halo_v, pooled_v, comp_v, s_v, g_v, p_v, rs_v,
    a_out, a_in, b_out, b_in, gp_v, carry_v,
    local_sem, pool_s, pool_r, part_s, part_r, rs_s, rs_r, a_s, a_r, b_s, b_r, side_sem,
):
    me = lax.axis_index("ctx")
    rows, count = t_v.shape
    nb = count // n
    inv = DH ** (-0.5)

    q_copy = pltpu.make_async_copy(q_hbm, q_v, local_sem.at[0])
    t_copy = pltpu.make_async_copy(t_hbm, t_v, local_sem.at[1])
    q_copy.start()
    t_copy.start()

    barrier = pltpu.get_barrier_semaphore()

    def greet(k, _):
        pl.semaphore_signal(
            barrier, inc=1, device_id={"ctx": lax.rem(me + k, n)},
            device_id_type=pl.DeviceIdType.MESH,
        )
        return 0

    lax.fori_loop(1, n, greet, 0)

    keys3 = keys_ref[...].astype(f32).reshape(nb, STRIDE, DH)
    gain_lo = gain_ref[0:STRIDE, :]
    gain_hi = gain_ref[STRIDE:KERNEL, :]
    low = jnp.sum(keys3 * gain_lo[None], axis=1)
    high = jnp.sum(keys3 * gain_hi[None], axis=1)
    pool_v[me] = (low + jnp.concatenate([high[1:], high[:1]], axis=0)).astype(bf16)
    part_v[me] = jnp.concatenate(
        [jnp.broadcast_to(low[nb - 1 : nb], (8, DH)), jnp.broadcast_to(high[0:1], (8, DH))], axis=0
    )
    part_v[n] = jnp.zeros((16, DH), f32)

    @pl.when(me == n - 1)
    def _():
        halo_v[...] = jnp.zeros((STRIDE, DH), bf16)

    @pl.when(me == 0)
    def _():
        carry_v[...] = jnp.zeros((8, DH), f32)

    pl.semaphore_wait(barrier, n - 1)

    def pool_copy(dst, slot):
        return remote(pool_v.at[slot], pool_v.at[slot], pool_s.at[dst], pool_r.at[slot], dst)

    def part_copy(dst, slot):
        return remote(part_v.at[slot], part_v.at[slot], part_s.at[dst], part_r.at[slot], dst)

    def send_pool(k, _):
        dst = lax.rem(me + k, n)
        pool_copy(dst, me).start()
        part_copy(dst, me).start()
        return 0

    lax.fori_loop(1, n, send_pool, 0)

    def halo_copy(dst):
        return remote(
            keys_ref.at[pl.ds(0, STRIDE)], halo_v, side_sem.at[0], side_sem.at[1], dst
        )

    @pl.when(me > 0)
    def _():
        halo_copy(me - 1).start()

    def take_pool(k, _):
        src = lax.rem(me + k, n)
        pool_copy(src, src).wait_recv()
        part_copy(src, src).wait_recv()
        return 0

    lax.fori_loop(1, n, take_pool, 0)
    last_row = lax.broadcasted_iota(jnp.int32, (nb, DH), 0) == nb - 1

    def place_pool(d, _):
        edge = part_v[d][0:1] + part_v[d + 1][8:9]
        block = jnp.where(last_row, edge, pool_v[d].astype(f32)).astype(bf16)
        at = pl.multiple_of(d * nb, nb)
        pooled_v[pl.ds(at, nb), :] = block
        comp_v[pl.ds(at, nb), :] = jnp.dot(
            block, w_ref[...], preferred_element_type=f32
        ).astype(bf16)
        return 0

    lax.fori_loop(0, n, place_pool, 0)
    q_copy.wait()
    t_copy.wait()

    place0 = slab_ref[0] * rows
    column_end = STRIDE * lax.broadcasted_iota(jnp.int32, (tr, count), 1) + (KERNEL - 1)
    row_in = lax.broadcasted_iota(jnp.int32, (tr, count), 0)
    nt = (((1,), (1,)), ((), ()))
    tn = (((0,), (0,)), ((), ()))

    def group(base, first, kl):
        rows_at = pl.ds(base, rb)
        for h in range(HEADS):
            qh = q_v[rows_at, h * DH : (h + 1) * DH]
            for c0 in range(0, count, CHUNK):
                s_v[h, :, c0 : c0 + CHUNK] = (
                    lax.dot_general(
                        qh, comp_v[c0 : c0 + CHUNK, :], nt, preferred_element_type=f32
                    )
                    * inv
                )

        def tile(i, kl):
            off = pl.multiple_of(i * tr, tr)
            here = pl.ds(off, tr)
            visible = column_end <= place0 + base + off + row_in
            top_all = jnp.full((tr, count), 2 * big_negative, f32)
            for h in range(HEADS):
                s = jnp.where(visible, s_v[h, here, :], big_negative)
                top = jnp.max(s, axis=1, keepdims=True)
                total = jnp.sum(jnp.exp(s - top), axis=1, keepdims=True)
                lse = jnp.where(top > 0.5 * big_negative, top + jnp.log(total), 0.0)
                x = s - lse
                s_v[h, here, :] = x
                top_all = jnp.maximum(top_all, x)
            mass = jnp.zeros((tr, count), f32)
            for h in range(HEADS):
                u = jnp.exp(s_v[h, here, :] - top_all)
                s_v[h, here, :] = u
                mass = mass + u
            teach = t_v[pl.ds(pl.multiple_of(base + off, tr), tr), :].astype(f32)
            seen = jnp.where(visible, teach, 0.0)
            teach_total = jnp.sum(seen, axis=1, keepdims=True)
            safe = jnp.where(teach_total > 0, teach_total, 1.0)
            tprob = seen / safe
            logm = jnp.where(visible, top_all + jnp.log(mass) - jnp.log(f32(HEADS)), 0.0)
            kl = kl + jnp.sum(
                tprob * (jnp.log(teach) - jnp.log(safe) - logm), axis=1, keepdims=True
            )
            weight = tprob / mass
            peak = jnp.exp(top_all)
            weight_s = loss_scale * weight
            for h in range(HEADS):
                u = s_v[h, here, :]
                cvec = loss_scale * jnp.sum(u * weight, axis=1, keepdims=True)
                g_v[h, here, :] = (u * (peak * cvec - weight_s)).astype(bf16)
            return kl

        kl = lax.fori_loop(0, rb // tr, tile, kl)
        for c0 in range(0, count, CHUNK):
            acc = jnp.zeros((DH, CHUNK), f32)
            for h in range(HEADS):
                acc = acc + lax.dot_general(
                    q_v[rows_at, h * DH : (h + 1) * DH], g_v[h, :, c0 : c0 + CHUNK], tn,
                    preferred_element_type=f32,
                )
            add = acc.T * inv
            if first is None:
                p_v[c0 : c0 + CHUNK, :] = add
            else:
                p_v[c0 : c0 + CHUNK, :] = p_v[c0 : c0 + CHUNK, :] + add
        return kl

    def query_grads(base):
        for h in range(HEADS):
            gq_v[pl.ds(base, rb), h * DH : (h + 1) * DH] = (
                jnp.dot(g_v[h], comp_v[...], preferred_element_type=f32) * inv
            ).astype(bf16)

    kl0 = jnp.zeros((tr, 1), f32)
    if rb == rows:
        kl = group(0, None, kl0)
    else:
        p_v[...] = jnp.zeros_like(p_v)

        def step(i, kl):
            base = pl.multiple_of(i * rb, rb)
            kl = group(base, False, kl)
            query_grads(base)
            return kl

        kl = lax.fori_loop(0, rows // rb, step, kl0)

    def rs_copy(dst, slot):
        at = pl.multiple_of(dst * nb, nb)
        return remote(p_v.at[pl.ds(at, nb)], rs_v.at[slot], rs_s.at[dst], rs_r.at[slot], dst)

    def send_rs(k, _):
        rs_copy(lax.rem(me + k, n), me).start()
        return 0

    lax.fori_loop(1, n, send_rs, 0)
    rs_v[me] = p_v[pl.ds(pl.multiple_of(me * nb, nb), nb), :]

    if rb == rows:
        query_grads(0)
    gq_copy = pltpu.make_async_copy(gq_v, gq_hbm, local_sem.at[2])
    gq_copy.start()

    @pl.when(me < n - 1)
    def _():
        halo_copy(me).wait_recv()

    upper3 = jnp.concatenate(
        [keys3[1:], halo_v[...].astype(f32).reshape(1, STRIDE, DH)], axis=0
    )

    def take_rs(k, _):
        rs_copy(lax.rem(me + k, n), lax.rem(me + k, n)).wait_recv()
        return 0

    lax.fori_loop(1, n, take_rs, 0)
    own = lax.fori_loop(1, n, lambda d, total: total + rs_v[d], rs_v[0])

    own3 = split3(own)
    gp3 = lax.dot_general(
        jnp.concatenate(own3, axis=0), w_ref[...], nt, preferred_element_type=f32
    )
    grad_pooled = (gp3[2 * nb :] + gp3[nb : 2 * nb]) + gp3[:nb]
    gp_v[...] = grad_pooled

    def carry_copy(dst):
        return remote(
            gp_v.at[pl.ds(nb - 8, 8)], carry_v, side_sem.at[2], side_sem.at[3], dst
        )

    @pl.when(me < n - 1)
    def _():
        carry_copy(me + 1).start()

    pooled_own = pooled_v[pl.ds(pl.multiple_of(me * nb, nb), nb), :]
    comp_part = lax.dot_general(
        jnp.concatenate([pooled_own] * 3, axis=0),
        jnp.concatenate(own3[::-1], axis=0),
        tn,
        preferred_element_type=f32,
    )
    gain_part = jnp.concatenate(
        [
            jnp.sum(grad_pooled[:, None, :] * keys3, axis=0),
            jnp.sum(grad_pooled[:, None, :] * upper3, axis=0),
        ],
        axis=0,
    )
    kl_row = jnp.broadcast_to(jnp.sum(kl, axis=0, keepdims=True), (1, DH))
    slot_rows = a_out.shape[1]
    for d in range(n):
        pieces = [comp_part[d * rc : (d + 1) * rc]]
        if (d + 1) * rg <= KERNEL:
            pieces.append(gain_part[d * rg : (d + 1) * rg])
        else:
            pieces.append(jnp.zeros((rg, DH), f32))
        pieces.append(jnp.broadcast_to(kl_row, (slot_rows - rc - rg, DH)))
        a_out[d] = jnp.concatenate(pieces, axis=0)

    def a_copy(dst, slot):
        return remote(a_out.at[dst], a_in.at[slot], a_s.at[dst], a_r.at[slot], dst)

    def send_a(k, _):
        a_copy(lax.rem(me + k, n), me).start()
        return 0

    lax.fori_loop(1, n, send_a, 0)
    a_in[me] = a_out[me]

    @pl.when(me > 0)
    def _():
        carry_copy(me).wait_recv()

    def take_a(k, _):
        a_copy(lax.rem(me + k, n), lax.rem(me + k, n)).wait_recv()
        return 0

    lax.fori_loop(1, n, take_a, 0)
    b_out[...] = lax.fori_loop(1, n, lambda d, total: total + a_in[d], a_in[0])

    def b_copy(dst, slot):
        return remote(b_out, b_in.at[slot], b_s.at[dst], b_r.at[slot], dst)

    def send_b(k, _):
        b_copy(lax.rem(me + k, n), me).start()
        return 0

    lax.fori_loop(1, n, send_b, 0)
    b_in[me] = b_out[...]
    loss_ref[...] = b_out[rc + rg : rc + rg + 1, :] * (1.0 / (rows * n))

    before = jnp.concatenate([carry_v[7:8, :], grad_pooled[: nb - 1]], axis=0)
    grad_keys = grad_pooled[:, None, :] * gain_lo[None] + before[:, None, :] * gain_hi[None]
    gk_ref[...] = grad_keys.reshape(nb * STRIDE, DH).astype(bf16)

    def drop_sends(k, _):
        dst = lax.rem(me + k, n)
        pool_copy(dst, me).wait_send()
        part_copy(dst, me).wait_send()
        rs_copy(dst, me).wait_send()
        a_copy(dst, me).wait_send()
        return 0

    lax.fori_loop(1, n, drop_sends, 0)

    @pl.when(me > 0)
    def _():
        halo_copy(me - 1).wait_send()

    @pl.when(me < n - 1)
    def _():
        carry_copy(me + 1).wait_send()

    def take_b(k, _):
        other = lax.rem(me + k, n)
        b_copy(other, other).wait_recv()
        b_copy(other, me).wait_send()
        return 0

    lax.fori_loop(1, n, take_b, 0)
    for d in range(n):
        gcomp_ref[d * rc : (d + 1) * rc, :] = b_in[d, 0:rc, :]
        if (d + 1) * rg <= KERNEL:
            ggain_ref[d * rg : (d + 1) * rg, :] = b_in[d, rc : rc + rg, :]
    gq_copy.wait()


def body(n, keys, queries, teacher_map, slab_index, pos_gain, w_comp):
    rows, count = teacher_map.shape
    nb = count // n
    rb = rows if count <= 1024 else 32
    tr = min(rb, 32 if count <= 1024 else 16)
    rc = -(-DH // n)
    rg = -(-KERNEL // n)
    slot_rows = -(-(rc + rg + 1) // 8) * 8
    dma = pltpu.SemaphoreType.DMA
    vmem = pl.BlockSpec(memory_space=pltpu.VMEM)
    hbm = pl.BlockSpec(memory_space=pl.ANY)
    loss, gq, gk, gcomp, ggain = pl.pallas_call(
        functools.partial(kernel, n, rb, tr, rc, rg),
        out_shape=(
            jax.ShapeDtypeStruct((1, DH), f32),
            jax.ShapeDtypeStruct((rows, HEADS * DH), bf16),
            jax.ShapeDtypeStruct(keys.shape, bf16),
            jax.ShapeDtypeStruct((DH, DH), f32),
            jax.ShapeDtypeStruct((KERNEL, DH), f32),
        ),
        in_specs=[pl.BlockSpec(memory_space=pltpu.SMEM), vmem, vmem, vmem, hbm, hbm],
        out_specs=(vmem, hbm, vmem, vmem, vmem),
        scratch_shapes=[
            pltpu.VMEM((rows, HEADS * DH), bf16),
            pltpu.VMEM((rows, count), bf16),
            pltpu.VMEM((rows, HEADS * DH), bf16),
            pltpu.VMEM((n, nb, DH), bf16),
            pltpu.VMEM((n + 1, 16, DH), f32),
            pltpu.VMEM((STRIDE, DH), bf16),
            pltpu.VMEM((count, DH), bf16),
            pltpu.VMEM((count, DH), bf16),
            pltpu.VMEM((HEADS, rb, count), f32),
            pltpu.VMEM((HEADS, rb, count), bf16),
            pltpu.VMEM((count, DH), f32),
            pltpu.VMEM((n, nb, DH), f32),
            pltpu.VMEM((n, slot_rows, DH), f32),
            pltpu.VMEM((n, slot_rows, DH), f32),
            pltpu.VMEM((slot_rows, DH), f32),
            pltpu.VMEM((n, slot_rows, DH), f32),
            pltpu.VMEM((nb, DH), f32),
            pltpu.VMEM((8, DH), f32),
            dma((3,)),
        ]
        + [dma((n,))] * 10
        + [dma((4,))],
        compiler_params=pltpu.CompilerParams(
            collective_id=0, has_side_effects=True, vmem_limit_bytes=48 * 1024 * 1024
        ),
    )(slab_index, keys, pos_gain, w_comp, queries, teacher_map)
    return (loss[0, 0:1], gq, gk, gcomp, ggain)


def solution(mesh):
    in_specs = (
        P(("groups", "ctx"), None),
        P(("groups", "ctx"), None),
        P(("groups", "ctx"), None),
        P(("groups", "ctx")),
        P(),
        P(),
    )
    out_specs = (
        P("groups"),
        P(("groups", "ctx"), None),
        P(("groups", "ctx"), None),
        P("groups", None),
        P("groups", None),
    )
    return jax.shard_map(
        functools.partial(body, mesh.shape["ctx"]),
        mesh=mesh, in_specs=in_specs, out_specs=out_specs, check_vma=False,
    )
```

```python
import functools

import jax
import jax.numpy as jnp
from jax import lax
from jax.experimental import pallas as pl
from jax.experimental.pallas import tpu as pltpu
from jax.sharding import PartitionSpec as P

DH = 128
HEADS = 8
KERNEL = 32
STRIDE = 16
CHUNK = 512

big_negative = -1e30
loss_scale = 256.0
f32 = jnp.float32
bf16 = jnp.bfloat16


def split3(x):
    first = x.astype(bf16)
    rest = x - first.astype(f32)
    second = rest.astype(bf16)
    third = (rest - second.astype(f32)).astype(bf16)
    return first, second, third


def remote(src, dst, send_sem, recv_sem, device):
    return pltpu.make_async_remote_copy(
        src_ref=src,
        dst_ref=dst,
        send_sem=send_sem,
        recv_sem=recv_sem,
        device_id={"ctx": device},
        device_id_type=pl.DeviceIdType.MESH,
    )


def kernel(
    n, rb, tr, rc, rg,
    slab_ref, keys_hbm, gain_hbm, w_hbm, q_hbm, t_hbm,
    loss_ref, gq_hbm, gk_ref, gcomp_ref, ggain_ref,
    keys_ref, gain_ref, w_ref, q_v, t_v, gq_v, pool_v, part_v, halo_v, pooled_v, comp_v, s_v, g_v, p_v, rs_v,
    a_out, a_in, b_out, b_in, gp_v, carry_v,
    local_sem, pool_s, pool_r, part_s, part_r, rs_s, rs_r, a_s, a_r, b_s, b_r, side_sem,
):
    me = lax.axis_index("ctx")
    rows, count = t_v.shape
    nb = count // n
    inv = DH ** (-0.5)

    q_copy = pltpu.make_async_copy(q_hbm, q_v, local_sem.at[0])
    t_copy = pltpu.make_async_copy(t_hbm, t_v, local_sem.at[1])
    keys_copy = pltpu.make_async_copy(keys_hbm, keys_ref, local_sem.at[3])
    gain_copy = pltpu.make_async_copy(gain_hbm, gain_ref, local_sem.at[4])
    w_copy = pltpu.make_async_copy(w_hbm, w_ref, local_sem.at[5])
    keys_copy.start()
    gain_copy.start()
    w_copy.start()
    q_copy.start()
    t_copy.start()

    barrier = pltpu.get_barrier_semaphore()

    def greet(k, _):
        pl.semaphore_signal(
            barrier, inc=1, device_id={"ctx": lax.rem(me + k, n)},
            device_id_type=pl.DeviceIdType.MESH,
        )
        return 0

    lax.fori_loop(1, n, greet, 0)

    keys_copy.wait()
    gain_copy.wait()
    keys3 = keys_ref[...].astype(f32).reshape(nb, STRIDE, DH)
    gain_lo = gain_ref[0:STRIDE, :]
    gain_hi = gain_ref[STRIDE:KERNEL, :]
    low = jnp.sum(keys3 * gain_lo[None], axis=1)
    high = jnp.sum(keys3 * gain_hi[None], axis=1)
    pool_v[me] = (low + jnp.concatenate([high[1:], high[:1]], axis=0)).astype(bf16)
    part_v[me, 0:1] = low[nb - 1 : nb]
    part_v[me, 1:2] = high[0:1]
    part_v[n] = jnp.zeros((8, DH), f32)

    @pl.when(me == n - 1)
    def _():
        halo_v[...] = jnp.zeros((STRIDE, DH), bf16)

    @pl.when(me == 0)
    def _():
        carry_v[...] = jnp.zeros((8, DH), f32)

    pl.semaphore_wait(barrier, n - 1)

    def pool_copy(dst, slot):
        return remote(pool_v.at[slot], pool_v.at[slot], pool_s.at[dst], pool_r.at[slot], dst)

    def part_copy(dst, slot):
        pair = part_v.at[slot, pl.ds(0, 2)]
        return remote(pair, pair, part_s.at[dst], part_r.at[slot], dst)

    def send_pool(k, _):
        dst = lax.rem(me + k, n)
        pool_copy(dst, me).start()
        part_copy(dst, me).start()
        return 0

    lax.fori_loop(1, n, send_pool, 0)

    def halo_copy(dst):
        return remote(
            keys_ref.at[pl.ds(0, STRIDE)], halo_v, side_sem.at[0], side_sem.at[1], dst
        )

    @pl.when(me > 0)
    def _():
        halo_copy(me - 1).start()

    def take_pool(k, _):
        src = lax.rem(me + k, n)
        pool_copy(src, src).wait_recv()
        part_copy(src, src).wait_recv()
        return 0

    lax.fori_loop(1, n, take_pool, 0)
    last_row = lax.broadcasted_iota(jnp.int32, (n, nb, DH), 1) == nb - 1
    edges = part_v[0:n, 0:1, :] + part_v[1 : n + 1, 1:2, :]
    pooled = jnp.where(last_row, edges, pool_v[...].astype(f32)).astype(bf16)
    pooled_v[...] = pooled.reshape(count, DH)
    w_copy.wait()
    comp_v[...] = jnp.dot(
        pooled_v[...], w_ref[...], preferred_element_type=f32
    ).astype(bf16)
    q_copy.wait()
    t_copy.wait()

    place0 = slab_ref[0] * rows
    column_end = STRIDE * lax.broadcasted_iota(jnp.int32, (tr, count), 1) + (KERNEL - 1)
    row_in = lax.broadcasted_iota(jnp.int32, (tr, count), 0)
    nt = (((1,), (1,)), ((), ()))
    tn = (((0,), (0,)), ((), ()))

    def group(base, first, kl):
        rows_at = pl.ds(base, rb)
        for h in range(HEADS):
            qh = q_v[rows_at, h * DH : (h + 1) * DH]
            for c0 in range(0, count, CHUNK):
                s_v[h, :, c0 : c0 + CHUNK] = (
                    lax.dot_general(
                        qh, comp_v[c0 : c0 + CHUNK, :], nt, preferred_element_type=f32
                    )
                    * inv
                )

        def tile(i, kl):
            off = pl.multiple_of(i * tr, tr)
            here = pl.ds(off, tr)
            visible = column_end <= place0 + base + off + row_in
            top_all = jnp.full((tr, count), 2 * big_negative, f32)
            for h in range(HEADS):
                s = jnp.where(visible, s_v[h, here, :], big_negative)
                top = jnp.max(s, axis=1, keepdims=True)
                total = jnp.sum(jnp.exp(s - top), axis=1, keepdims=True)
                lse = jnp.where(top > 0.5 * big_negative, top + jnp.log(total), 0.0)
                x = s - lse
                s_v[h, here, :] = x
                top_all = jnp.maximum(top_all, x)
            mass = jnp.zeros((tr, count), f32)
            for h in range(HEADS):
                u = jnp.exp(s_v[h, here, :] - top_all)
                s_v[h, here, :] = u
                mass = mass + u
            teach = t_v[pl.ds(pl.multiple_of(base + off, tr), tr), :].astype(f32)
            seen = jnp.where(visible, teach, 0.0)
            teach_total = jnp.sum(seen, axis=1, keepdims=True)
            safe = jnp.where(teach_total > 0, teach_total, 1.0)
            tprob = seen / safe
            logm = jnp.where(visible, top_all + jnp.log(mass) - jnp.log(f32(HEADS)), 0.0)
            kl = kl + jnp.sum(
                tprob * (jnp.log(teach) - jnp.log(safe) - logm), axis=1, keepdims=True
            )
            weight = tprob / mass
            peak = jnp.exp(top_all)
            weight_s = loss_scale * weight
            for h in range(HEADS):
                u = s_v[h, here, :]
                cvec = loss_scale * jnp.sum(u * weight, axis=1, keepdims=True)
                g_v[h, here, :] = (u * (peak * cvec - weight_s)).astype(bf16)
            return kl

        kl = lax.fori_loop(0, rb // tr, tile, kl)
        for c0 in range(0, count, CHUNK):
            acc = jnp.zeros((DH, CHUNK), f32)
            for h in range(HEADS):
                acc = acc + lax.dot_general(
                    q_v[rows_at, h * DH : (h + 1) * DH], g_v[h, :, c0 : c0 + CHUNK], tn,
                    preferred_element_type=f32,
                )
            add = acc.T * inv
            if first is None:
                p_v[c0 : c0 + CHUNK, :] = add
            else:
                p_v[c0 : c0 + CHUNK, :] = p_v[c0 : c0 + CHUNK, :] + add
        return kl

    def query_grads(base):
        for h in range(HEADS):
            gq_v[pl.ds(base, rb), h * DH : (h + 1) * DH] = (
                jnp.dot(g_v[h], comp_v[...], preferred_element_type=f32) * inv
            ).astype(bf16)

    kl0 = jnp.zeros((tr, 1), f32)
    if rb == rows:
        kl = group(0, None, kl0)
    else:
        p_v[...] = jnp.zeros_like(p_v)

        def step(i, kl):
            base = pl.multiple_of(i * rb, rb)
            kl = group(base, False, kl)
            query_grads(base)
            return kl

        kl = lax.fori_loop(0, rows // rb, step, kl0)

    def rs_copy(dst, slot):
        at = pl.multiple_of(dst * nb, nb)
        return remote(p_v.at[pl.ds(at, nb)], rs_v.at[slot], rs_s.at[dst], rs_r.at[slot], dst)

    def send_rs(k, _):
        rs_copy(lax.rem(me + k, n), me).start()
        return 0

    lax.fori_loop(1, n, send_rs, 0)
    rs_v[me] = p_v[pl.ds(pl.multiple_of(me * nb, nb), nb), :]

    if rb == rows:
        query_grads(0)
    gq_copy = pltpu.make_async_copy(gq_v, gq_hbm, local_sem.at[2])
    gq_copy.start()

    @pl.when(me < n - 1)
    def _():
        halo_copy(me).wait_recv()

    upper3 = jnp.concatenate(
        [keys3[1:], halo_v[...].astype(f32).reshape(1, STRIDE, DH)], axis=0
    )

    def take_rs(k, _):
        rs_copy(lax.rem(me + k, n), lax.rem(me + k, n)).wait_recv()
        return 0

    lax.fori_loop(1, n, take_rs, 0)
    own = lax.fori_loop(1, n, lambda d, total: total + rs_v[d], rs_v[0])

    own3 = split3(own)
    gp3 = lax.dot_general(
        jnp.concatenate(own3, axis=0), w_ref[...], nt, preferred_element_type=f32
    )
    grad_pooled = (gp3[2 * nb :] + gp3[nb : 2 * nb]) + gp3[:nb]
    gp_v[...] = grad_pooled

    def carry_copy(dst):
        return remote(
            gp_v.at[pl.ds(nb - 8, 8)], carry_v, side_sem.at[2], side_sem.at[3], dst
        )

    @pl.when(me < n - 1)
    def _():
        carry_copy(me + 1).start()

    pooled_own = pooled_v[pl.ds(pl.multiple_of(me * nb, nb), nb), :]
    comp_part = lax.dot_general(
        jnp.concatenate([pooled_own] * 3, axis=0),
        jnp.concatenate(own3[::-1], axis=0),
        tn,
        preferred_element_type=f32,
    )
    gain_part = jnp.concatenate(
        [
            jnp.sum(grad_pooled[:, None, :] * keys3, axis=0),
            jnp.sum(grad_pooled[:, None, :] * upper3, axis=0),
        ],
        axis=0,
    )
    kl_row = jnp.broadcast_to(jnp.sum(kl, axis=0, keepdims=True), (1, DH))
    slot_rows = a_out.shape[1]
    for d in range(n):
        pieces = [comp_part[d * rc : (d + 1) * rc]]
        if (d + 1) * rg <= KERNEL:
            pieces.append(gain_part[d * rg : (d + 1) * rg])
        else:
            pieces.append(jnp.zeros((rg, DH), f32))
        pieces.append(jnp.broadcast_to(kl_row, (slot_rows - rc - rg, DH)))
        a_out[d] = jnp.concatenate(pieces, axis=0)

    def a_copy(dst, slot):
        used = pl.ds(0, rc + rg + 1)
        return remote(
            a_out.at[dst, used], a_in.at[slot, used], a_s.at[dst], a_r.at[slot], dst
        )

    def send_a(k, _):
        a_copy(lax.rem(me + k, n), me).start()
        return 0

    lax.fori_loop(1, n, send_a, 0)
    a_in[me] = a_out[me]

    @pl.when(me > 0)
    def _():
        carry_copy(me).wait_recv()

    def take_a(k, _):
        a_copy(lax.rem(me + k, n), lax.rem(me + k, n)).wait_recv()
        return 0

    lax.fori_loop(1, n, take_a, 0)
    b_out[...] = lax.fori_loop(1, n, lambda d, total: total + a_in[d], a_in[0])

    def b_copy(dst, slot):
        used = pl.ds(0, rc + rg)
        return remote(
            b_out.at[used], b_in.at[slot, used], b_s.at[dst], b_r.at[slot], dst
        )

    def send_b(k, _):
        b_copy(lax.rem(me + k, n), me).start()
        return 0

    lax.fori_loop(1, n, send_b, 0)
    b_in[me] = b_out[...]
    loss_ref[...] = b_out[rc + rg : rc + rg + 1, :] * (1.0 / (rows * n))

    before = jnp.concatenate([carry_v[7:8, :], grad_pooled[: nb - 1]], axis=0)
    grad_keys = grad_pooled[:, None, :] * gain_lo[None] + before[:, None, :] * gain_hi[None]
    gk_ref[...] = grad_keys.reshape(nb * STRIDE, DH).astype(bf16)

    def drop_sends(k, _):
        dst = lax.rem(me + k, n)
        pool_copy(dst, me).wait_send()
        part_copy(dst, me).wait_send()
        rs_copy(dst, me).wait_send()
        a_copy(dst, me).wait_send()
        return 0

    lax.fori_loop(1, n, drop_sends, 0)

    @pl.when(me > 0)
    def _():
        halo_copy(me - 1).wait_send()

    @pl.when(me < n - 1)
    def _():
        carry_copy(me + 1).wait_send()

    def take_b(k, _):
        other = lax.rem(me + k, n)
        b_copy(other, other).wait_recv()
        b_copy(other, me).wait_send()
        return 0

    lax.fori_loop(1, n, take_b, 0)
    for d in range(n):
        gcomp_ref[d * rc : (d + 1) * rc, :] = b_in[d, 0:rc, :]
        if (d + 1) * rg <= KERNEL:
            ggain_ref[d * rg : (d + 1) * rg, :] = b_in[d, rc : rc + rg, :]
    gq_copy.wait()


def finish(*refs):
    sources, targets, sem = refs[:5], refs[5:10], refs[10]
    copies = [
        pltpu.make_async_copy(source, target, sem.at[i])
        for i, (source, target) in enumerate(zip(sources, targets))
    ]
    for copy in copies:
        copy.start()
    for copy in copies:
        copy.wait()


def body(n, keys, queries, teacher_map, slab_index, pos_gain, w_comp):
    rows, count = teacher_map.shape
    nb = count // n
    rb = rows if count <= 1024 else 32
    tr = min(rb, 32 if count <= 1024 else 16)
    rc = -(-DH // n)
    rg = -(-KERNEL // n)
    slot_rows = -(-(rc + rg + 1) // 8) * 8
    dma = pltpu.SemaphoreType.DMA
    vmem = pl.BlockSpec(memory_space=pltpu.VMEM)
    hbm = pl.BlockSpec(memory_space=pltpu.HBM)
    shapes = (
            jax.ShapeDtypeStruct((1, DH), f32),
            jax.ShapeDtypeStruct((rows, HEADS * DH), bf16),
            jax.ShapeDtypeStruct(keys.shape, bf16),
            jax.ShapeDtypeStruct((DH, DH), f32),
            jax.ShapeDtypeStruct((KERNEL, DH), f32),
        )
    results = pl.pallas_call(
        functools.partial(kernel, n, rb, tr, rc, rg),
        out_shape=shapes,
        in_specs=[pl.BlockSpec(memory_space=pltpu.SMEM)] + [hbm] * 5,
        out_specs=(vmem, hbm, vmem, vmem, vmem),
        scratch_shapes=[
            pltpu.VMEM(keys.shape, bf16),
            pltpu.VMEM(pos_gain.shape, f32),
            pltpu.VMEM(w_comp.shape, bf16),
            pltpu.VMEM((rows, HEADS * DH), bf16),
            pltpu.VMEM((rows, count), bf16),
            pltpu.VMEM((rows, HEADS * DH), bf16),
            pltpu.VMEM((n, nb, DH), bf16),
            pltpu.VMEM((n + 1, 8, DH), f32),
            pltpu.VMEM((STRIDE, DH), bf16),
            pltpu.VMEM((count, DH), bf16),
            pltpu.VMEM((count, DH), bf16),
            pltpu.VMEM((HEADS, rb, count), f32),
            pltpu.VMEM((HEADS, rb, count), bf16),
            pltpu.VMEM((count, DH), f32),
            pltpu.VMEM((n, nb, DH), f32),
            pltpu.VMEM((n, slot_rows, DH), f32),
            pltpu.VMEM((n, slot_rows, DH), f32),
            pltpu.VMEM((slot_rows, DH), f32),
            pltpu.VMEM((n, slot_rows, DH), f32),
            pltpu.VMEM((nb, DH), f32),
            pltpu.VMEM((8, DH), f32),
            dma((6,)),
        ]
        + [dma((n,))] * 10
        + [dma((4,))],
        compiler_params=pltpu.CompilerParams(
            collective_id=0, has_side_effects=True, vmem_limit_bytes=48 * 1024 * 1024
        ),
    )(slab_index, *[pltpu.with_memory_space_constraint(x, pltpu.HBM) for x in (keys, pos_gain, w_comp, queries, teacher_map)])
    any_space = pl.BlockSpec(memory_space=pl.ANY)
    loss, gq, gk, gcomp, ggain = pl.pallas_call(
        finish,
        out_shape=shapes,
        in_specs=[any_space] * 5,
        out_specs=[any_space] * 5,
        scratch_shapes=[dma((5,))],
        compiler_params=pltpu.CompilerParams(vmem_limit_bytes=4 * 1024 * 1024),
    )(*results)
    return (loss[0, 0:1], gq, gk, gcomp, ggain)


def solution(mesh):
    in_specs = (
        P(("groups", "ctx"), None),
        P(("groups", "ctx"), None),
        P(("groups", "ctx"), None),
        P(("groups", "ctx")),
        P(),
        P(),
    )
    out_specs = (
        P("groups"),
        P(("groups", "ctx"), None),
        P(("groups", "ctx"), None),
        P("groups", None),
        P("groups", None),
    )
    return jax.shard_map(
        functools.partial(body, mesh.shape["ctx"]),
        mesh=mesh, in_specs=in_specs, out_specs=out_specs, check_vma=False,
    )
```

```python
import functools

import jax
import jax.numpy as jnp
from jax import lax
from jax.experimental import pallas as pl
from jax.experimental.pallas import tpu as pltpu
from jax.sharding import PartitionSpec as P

DH = 128
HEADS = 8
KERNEL = 32
STRIDE = 16
CHUNK = 512

big_negative = -1e30
loss_scale = 256.0
f32 = jnp.float32
bf16 = jnp.bfloat16


def split3(x):
    first = x.astype(bf16)
    rest = x - first.astype(f32)
    second = rest.astype(bf16)
    third = (rest - second.astype(f32)).astype(bf16)
    return first, second, third


def remote(src, dst, send_sem, recv_sem, device):
    return pltpu.make_async_remote_copy(
        src_ref=src,
        dst_ref=dst,
        send_sem=send_sem,
        recv_sem=recv_sem,
        device_id={"ctx": device},
        device_id_type=pl.DeviceIdType.MESH,
    )


def kernel(
    n, rb, tr, rc, rg,
    slab_ref, keys_hbm, gain_hbm, w_hbm, q_hbm, t_hbm,
    loss_ref, gq_hbm, gk_ref, gcomp_ref, ggain_ref,
    keys_ref, gain_ref, w_ref, q_v, t_v, gq_v, pool_v, part_v, halo_v, pooled_v, comp_v, s_v, g_v, p_v, pair_v, rs_v,
    a_out, a_in, b_out, b_in, gp_v, carry_v,
    local_sem, pool_s, pool_r, part_s, part_r, pair_s, pair_r, rs_s, rs_r, a_s, a_r, b_s, b_r, side_sem,
):
    me = lax.axis_index("ctx")
    rows, count = t_v.shape
    nb = count // n
    inv = DH ** (-0.5)

    barrier = pltpu.get_barrier_semaphore()

    def greet(k, _):
        pl.semaphore_signal(
            barrier, inc=1, device_id={"ctx": lax.rem(me + k, n)},
            device_id_type=pl.DeviceIdType.MESH,
        )
        return 0

    lax.fori_loop(1, n, greet, 0)

    q_copy = pltpu.make_async_copy(q_hbm, q_v, local_sem.at[0])
    t_copy = pltpu.make_async_copy(t_hbm, t_v, local_sem.at[1])
    keys_copy = pltpu.make_async_copy(keys_hbm, keys_ref, local_sem.at[3])
    gain_copy = pltpu.make_async_copy(gain_hbm, gain_ref, local_sem.at[4])
    w_copy = pltpu.make_async_copy(w_hbm, w_ref, local_sem.at[5])
    keys_copy.start()
    gain_copy.start()
    w_copy.start()
    q_copy.start()
    t_copy.start()

    keys_copy.wait()
    gain_copy.wait()
    keys3 = keys_ref[...].astype(f32).reshape(nb, STRIDE, DH)
    gain_lo = gain_ref[0:STRIDE, :]
    gain_hi = gain_ref[STRIDE:KERNEL, :]
    low = jnp.sum(keys3 * gain_lo[None], axis=1)
    high = jnp.sum(keys3 * gain_hi[None], axis=1)
    pool_v[me] = (low + jnp.concatenate([high[1:], high[:1]], axis=0)).astype(bf16)
    part_v[me, 0:1] = low[nb - 1 : nb]
    part_v[me, 1:2] = high[0:1]
    part_v[n] = jnp.zeros((8, DH), f32)

    @pl.when(me == n - 1)
    def _():
        halo_v[...] = jnp.zeros((STRIDE, DH), bf16)

    @pl.when(me == 0)
    def _():
        carry_v[...] = jnp.zeros((8, DH), f32)

    pl.semaphore_wait(barrier, n - 1)

    def pool_copy(dst, slot):
        return remote(pool_v.at[slot], pool_v.at[slot], pool_s.at[dst], pool_r.at[slot], dst)

    def part_copy(dst, slot):
        pair = part_v.at[slot, pl.ds(0, 2)]
        return remote(pair, pair, part_s.at[dst], part_r.at[slot], dst)

    def send_pool(k, _):
        dst = lax.rem(me + k, n)
        pool_copy(dst, me).start()
        part_copy(dst, me).start()
        return 0

    lax.fori_loop(1, n, send_pool, 0)

    def halo_copy(dst):
        return remote(
            keys_ref.at[pl.ds(0, STRIDE)], halo_v, side_sem.at[0], side_sem.at[1], dst
        )

    @pl.when(me > 0)
    def _():
        halo_copy(me - 1).start()

    def take_pool(k, _):
        src = lax.rem(me + k, n)
        pool_copy(src, src).wait_recv()
        part_copy(src, src).wait_recv()
        return 0

    lax.fori_loop(1, n, take_pool, 0)
    last_row = lax.broadcasted_iota(jnp.int32, (n, nb, DH), 1) == nb - 1
    edges = part_v[0:n, 0:1, :] + part_v[1 : n + 1, 1:2, :]
    pooled = jnp.where(last_row, edges, pool_v[...].astype(f32)).astype(bf16)
    pooled_v[...] = pooled.reshape(count, DH)
    w_copy.wait()
    comp_v[...] = jnp.dot(
        pooled_v[...], w_ref[...], preferred_element_type=f32
    ).astype(bf16)
    q_copy.wait()
    t_copy.wait()

    place0 = slab_ref[0] * rows
    column_end = STRIDE * lax.broadcasted_iota(jnp.int32, (tr, count), 1) + (KERNEL - 1)
    row_in = lax.broadcasted_iota(jnp.int32, (tr, count), 0)
    nt = (((1,), (1,)), ((), ()))
    tn = (((0,), (0,)), ((), ()))

    def group(base, first, kl):
        rows_at = pl.ds(base, rb)
        for h in range(HEADS):
            qh = q_v[rows_at, h * DH : (h + 1) * DH]
            for c0 in range(0, count, CHUNK):
                s_v[h, :, c0 : c0 + CHUNK] = (
                    lax.dot_general(
                        qh, comp_v[c0 : c0 + CHUNK, :], nt, preferred_element_type=f32
                    )
                    * inv
                )

        def tile(i, kl):
            off = pl.multiple_of(i * tr, tr)
            here = pl.ds(off, tr)
            visible = column_end <= place0 + base + off + row_in
            top_all = jnp.full((tr, count), 2 * big_negative, f32)
            for h in range(HEADS):
                s = jnp.where(visible, s_v[h, here, :], big_negative)
                top = jnp.max(s, axis=1, keepdims=True)
                total = jnp.sum(jnp.exp(s - top), axis=1, keepdims=True)
                lse = jnp.where(top > 0.5 * big_negative, top + jnp.log(total), 0.0)
                x = s - lse
                s_v[h, here, :] = x
                top_all = jnp.maximum(top_all, x)
            mass = jnp.zeros((tr, count), f32)
            for h in range(HEADS):
                u = jnp.exp(s_v[h, here, :] - top_all)
                s_v[h, here, :] = u
                mass = mass + u
            teach = t_v[pl.ds(pl.multiple_of(base + off, tr), tr), :].astype(f32)
            seen = jnp.where(visible, teach, 0.0)
            teach_total = jnp.sum(seen, axis=1, keepdims=True)
            safe = jnp.where(teach_total > 0, teach_total, 1.0)
            tprob = seen / safe
            logm = jnp.where(visible, top_all + jnp.log(mass) - jnp.log(f32(HEADS)), 0.0)
            kl = kl + jnp.sum(
                tprob * (jnp.log(teach) - jnp.log(safe) - logm), axis=1, keepdims=True
            )
            weight = tprob / mass
            peak = jnp.exp(top_all)
            weight_s = loss_scale * weight
            for h in range(HEADS):
                u = s_v[h, here, :]
                cvec = loss_scale * jnp.sum(u * weight, axis=1, keepdims=True)
                g_v[h, here, :] = (u * (peak * cvec - weight_s)).astype(bf16)
            return kl

        kl = lax.fori_loop(0, rb // tr, tile, kl)
        for c0 in range(0, count, CHUNK):
            acc = jnp.zeros((DH, CHUNK), f32)
            for h in range(HEADS):
                acc = acc + lax.dot_general(
                    q_v[rows_at, h * DH : (h + 1) * DH], g_v[h, :, c0 : c0 + CHUNK], tn,
                    preferred_element_type=f32,
                )
            add = acc.T * inv
            for r0 in range(0, CHUNK, nb):
                owner = (c0 + r0) // nb
                at = (owner % 2, owner // 2)
                if first is None:
                    p_v[at] = add[r0 : r0 + nb]
                else:
                    p_v[at] = p_v[at] + add[r0 : r0 + nb]
        return kl

    def query_grads(base):
        for h in range(HEADS):
            gq_v[pl.ds(base, rb), h * DH : (h + 1) * DH] = (
                jnp.dot(g_v[h], comp_v[...], preferred_element_type=f32) * inv
            ).astype(bf16)

    kl0 = jnp.zeros((tr, 1), f32)
    if rb == rows:
        kl = group(0, None, kl0)
    else:
        p_v[...] = jnp.zeros_like(p_v)

        def step(i, kl):
            base = pl.multiple_of(i * rb, rb)
            kl = group(base, False, kl)
            query_grads(base)
            return kl

        kl = lax.fori_loop(0, rows // rb, step, kl0)

    core = lax.rem(me, 2)
    mine = lax.div(me, 2)
    half = n // 2
    twin = me + 1 - 2 * core

    def pair_copy(slot):
        return remote(
            p_v.at[1 - core, slot], pair_v.at[slot], pair_s.at[slot], pair_r.at[slot], twin
        )

    def rs_copy(dst, slot):
        return remote(
            p_v.at[core, dst], rs_v.at[slot], rs_s.at[dst], rs_r.at[slot], 2 * dst + core
        )

    def send_pair(k, _):
        pair_copy(lax.rem(mine + k, half)).start()
        return 0

    lax.fori_loop(1, half + 1, send_pair, 0)

    def forward(k, _):
        slot = lax.rem(mine + k, half)
        pair_copy(slot).wait_recv()
        p_v[core, slot] = p_v[core, slot] + pair_v[slot]
        rs_copy(slot, mine).start()
        return 0

    lax.fori_loop(1, half, forward, 0)
    pair_copy(mine).wait_recv()
    rs_v[mine] = p_v[core, mine] + pair_v[mine]

    if rb == rows:
        query_grads(0)
    gq_copy = pltpu.make_async_copy(gq_v, gq_hbm, local_sem.at[2])
    gq_copy.start()

    @pl.when(me < n - 1)
    def _():
        halo_copy(me).wait_recv()

    upper3 = jnp.concatenate(
        [keys3[1:], halo_v[...].astype(f32).reshape(1, STRIDE, DH)], axis=0
    )

    def take_rs(k, _):
        slot = lax.rem(mine + k, half)
        rs_copy(slot, slot).wait_recv()
        return 0

    lax.fori_loop(1, half, take_rs, 0)
    own = lax.fori_loop(1, half, lambda d, total: total + rs_v[d], rs_v[0])

    own3 = split3(own)
    gp3 = lax.dot_general(
        jnp.concatenate(own3, axis=0), w_ref[...], nt, preferred_element_type=f32
    )
    grad_pooled = (gp3[2 * nb :] + gp3[nb : 2 * nb]) + gp3[:nb]
    gp_v[...] = grad_pooled

    def carry_copy(dst):
        return remote(
            gp_v.at[pl.ds(nb - 8, 8)], carry_v, side_sem.at[2], side_sem.at[3], dst
        )

    @pl.when(me < n - 1)
    def _():
        carry_copy(me + 1).start()

    pooled_own = pooled_v[pl.ds(pl.multiple_of(me * nb, nb), nb), :]
    comp_part = lax.dot_general(
        jnp.concatenate([pooled_own] * 3, axis=0),
        jnp.concatenate(own3[::-1], axis=0),
        tn,
        preferred_element_type=f32,
    )
    gain_part = jnp.concatenate(
        [
            jnp.sum(grad_pooled[:, None, :] * keys3, axis=0),
            jnp.sum(grad_pooled[:, None, :] * upper3, axis=0),
        ],
        axis=0,
    )
    kl_row = jnp.broadcast_to(jnp.sum(kl, axis=0, keepdims=True), (1, DH))
    slot_rows = a_out.shape[1]
    for d in range(n):
        pieces = [comp_part[d * rc : (d + 1) * rc]]
        if (d + 1) * rg <= KERNEL:
            pieces.append(gain_part[d * rg : (d + 1) * rg])
        else:
            pieces.append(jnp.zeros((rg, DH), f32))
        pieces.append(jnp.broadcast_to(kl_row, (slot_rows - rc - rg, DH)))
        a_out[d] = jnp.concatenate(pieces, axis=0)

    def a_copy(dst, slot):
        used = pl.ds(0, rc + rg + 1)
        return remote(
            a_out.at[dst, used], a_in.at[slot, used], a_s.at[dst], a_r.at[slot], dst
        )

    def send_a(k, _):
        a_copy(lax.rem(me + k, n), me).start()
        return 0

    lax.fori_loop(1, n, send_a, 0)
    a_in[me] = a_out[me]

    @pl.when(me > 0)
    def _():
        carry_copy(me).wait_recv()

    def take_a(k, _):
        a_copy(lax.rem(me + k, n), lax.rem(me + k, n)).wait_recv()
        return 0

    lax.fori_loop(1, n, take_a, 0)
    b_out[...] = lax.fori_loop(1, n, lambda d, total: total + a_in[d], a_in[0])

    def b_copy(dst, slot):
        used = pl.ds(0, rc + rg)
        return remote(
            b_out.at[used], b_in.at[slot, used], b_s.at[dst], b_r.at[slot], dst
        )

    def send_b(k, _):
        b_copy(lax.rem(me + k, n), me).start()
        return 0

    lax.fori_loop(1, n, send_b, 0)
    b_in[me] = b_out[...]
    loss_ref[...] = b_out[rc + rg : rc + rg + 1, :] * (1.0 / (rows * n))

    before = jnp.concatenate([carry_v[7:8, :], grad_pooled[: nb - 1]], axis=0)
    grad_keys = grad_pooled[:, None, :] * gain_lo[None] + before[:, None, :] * gain_hi[None]
    gk_ref[...] = grad_keys.reshape(nb * STRIDE, DH).astype(bf16)

    def drop_sends(k, _):
        dst = lax.rem(me + k, n)
        pool_copy(dst, me).wait_send()
        part_copy(dst, me).wait_send()
        a_copy(dst, me).wait_send()
        return 0

    lax.fori_loop(1, n, drop_sends, 0)

    def drop_pairs(k, _):
        slot = lax.rem(mine + k, half)
        pair_copy(slot).wait_send()
        rs_copy(slot, mine).wait_send()
        return 0

    lax.fori_loop(1, half, drop_pairs, 0)
    pair_copy(mine).wait_send()

    @pl.when(me > 0)
    def _():
        halo_copy(me - 1).wait_send()

    @pl.when(me < n - 1)
    def _():
        carry_copy(me + 1).wait_send()

    def take_b(k, _):
        other = lax.rem(me + k, n)
        b_copy(other, other).wait_recv()
        b_copy(other, me).wait_send()
        return 0

    lax.fori_loop(1, n, take_b, 0)
    for d in range(n):
        gcomp_ref[d * rc : (d + 1) * rc, :] = b_in[d, 0:rc, :]
        if (d + 1) * rg <= KERNEL:
            ggain_ref[d * rg : (d + 1) * rg, :] = b_in[d, rc : rc + rg, :]
    gq_copy.wait()


def finish(*refs):
    sources, targets, sem = refs[:5], refs[5:10], refs[10]
    copies = [
        pltpu.make_async_copy(source, target, sem.at[i])
        for i, (source, target) in enumerate(zip(sources, targets))
    ]
    for copy in copies:
        copy.start()
    for copy in copies:
        copy.wait()


def body(n, keys, queries, teacher_map, slab_index, pos_gain, w_comp):
    rows, count = teacher_map.shape
    nb = count // n
    rb = rows if count <= 1024 else 32
    tr = min(rb, 64 if count <= 1024 else 16)
    rc = -(-DH // n)
    rg = -(-KERNEL // n)
    slot_rows = -(-(rc + rg + 1) // 8) * 8
    dma = pltpu.SemaphoreType.DMA
    vmem = pl.BlockSpec(memory_space=pltpu.VMEM)
    hbm = pl.BlockSpec(memory_space=pltpu.HBM)
    shapes = (
            jax.ShapeDtypeStruct((1, DH), f32),
            jax.ShapeDtypeStruct((rows, HEADS * DH), bf16),
            jax.ShapeDtypeStruct(keys.shape, bf16),
            jax.ShapeDtypeStruct((DH, DH), f32),
            jax.ShapeDtypeStruct((KERNEL, DH), f32),
        )
    results = pl.pallas_call(
        functools.partial(kernel, n, rb, tr, rc, rg),
        out_shape=shapes,
        in_specs=[pl.BlockSpec(memory_space=pltpu.SMEM)] + [hbm] * 5,
        out_specs=(vmem, hbm, vmem, vmem, vmem),
        scratch_shapes=[
            pltpu.VMEM(keys.shape, bf16),
            pltpu.VMEM(pos_gain.shape, f32),
            pltpu.VMEM(w_comp.shape, bf16),
            pltpu.VMEM((rows, HEADS * DH), bf16),
            pltpu.VMEM((rows, count), bf16),
            pltpu.VMEM((rows, HEADS * DH), bf16),
            pltpu.VMEM((n, nb, DH), bf16),
            pltpu.VMEM((n + 1, 8, DH), f32),
            pltpu.VMEM((STRIDE, DH), bf16),
            pltpu.VMEM((count, DH), bf16),
            pltpu.VMEM((count, DH), bf16),
            pltpu.VMEM((HEADS, rb, count), f32),
            pltpu.VMEM((HEADS, rb, count), bf16),
            pltpu.VMEM((2, n // 2, nb, DH), f32),
            pltpu.VMEM((n // 2, nb, DH), f32),
            pltpu.VMEM((n // 2, nb, DH), f32),
            pltpu.VMEM((n, slot_rows, DH), f32),
            pltpu.VMEM((n, slot_rows, DH), f32),
            pltpu.VMEM((slot_rows, DH), f32),
            pltpu.VMEM((n, slot_rows, DH), f32),
            pltpu.VMEM((nb, DH), f32),
            pltpu.VMEM((8, DH), f32),
            dma((6,)),
        ]
        + [dma((n,))] * 4
        + [dma((n // 2,))] * 4
        + [dma((n,))] * 4
        + [dma((4,))],
        compiler_params=pltpu.CompilerParams(
            collective_id=0, has_side_effects=True, vmem_limit_bytes=48 * 1024 * 1024
        ),
    )(slab_index, *[pltpu.with_memory_space_constraint(x, pltpu.HBM) for x in (keys, pos_gain, w_comp, queries, teacher_map)])
    any_space = pl.BlockSpec(memory_space=pl.ANY)
    loss, gq, gk, gcomp, ggain = pl.pallas_call(
        finish,
        out_shape=shapes,
        in_specs=[any_space] * 5,
        out_specs=[any_space] * 5,
        scratch_shapes=[dma((5,))],
        compiler_params=pltpu.CompilerParams(vmem_limit_bytes=4 * 1024 * 1024),
    )(*results)
    return (loss[0, 0:1], gq, gk, gcomp, ggain)


def solution(mesh):
    in_specs = (
        P(("groups", "ctx"), None),
        P(("groups", "ctx"), None),
        P(("groups", "ctx"), None),
        P(("groups", "ctx")),
        P(),
        P(),
    )
    out_specs = (
        P("groups"),
        P(("groups", "ctx"), None),
        P(("groups", "ctx"), None),
        P("groups", None),
        P("groups", None),
    )
    return jax.shard_map(
        functools.partial(body, mesh.shape["ctx"]),
        mesh=mesh, in_specs=in_specs, out_specs=out_specs, check_vma=False,
    )
```

```python
import functools

import jax
import jax.numpy as jnp
from jax import lax
from jax.experimental import pallas as pl
from jax.experimental.pallas import tpu as pltpu
from jax.sharding import PartitionSpec as P

DH = 128
HEADS = 8
KERNEL = 32
STRIDE = 16
CHUNK = 256

big_negative = -1e30
loss_scale = 256.0
f32 = jnp.float32
bf16 = jnp.bfloat16


def split3(x):
    first = x.astype(bf16)
    rest = x - first.astype(f32)
    second = rest.astype(bf16)
    third = (rest - second.astype(f32)).astype(bf16)
    return first, second, third


def remote(src, dst, send_sem, recv_sem, device):
    return pltpu.make_async_remote_copy(
        src_ref=src,
        dst_ref=dst,
        send_sem=send_sem,
        recv_sem=recv_sem,
        device_id={"ctx": device},
        device_id_type=pl.DeviceIdType.MESH,
    )


def kernel(
    n, rb, tr, rc, rg,
    slab_ref, keys_hbm, gain_hbm, w_hbm, q_hbm, t_hbm,
    loss_ref, gq_ref, gk_ref, gcomp_ref, ggain_ref,
    keys_ref, gain_ref, w_ref, q_v, t_v, pool_v, part_v, halo_v, pooled_v, comp_v, s_v, g_v, p_v, pair_v, rs_v,
    a_out, a_in, b_out, b_in, gp_v, carry_v,
    local_sem, pool_s, pool_r, part_s, part_r, pair_s, pair_r, rs_s, rs_r, a_s, a_r, b_s, b_r, side_sem,
):
    me = lax.axis_index("ctx")
    rows, count = t_v.shape
    nb = count // n
    inv = DH ** (-0.5)

    barrier = pltpu.get_barrier_semaphore()

    def greet(k, _):
        pl.semaphore_signal(
            barrier, inc=1, device_id={"ctx": lax.rem(me + k, n)},
            device_id_type=pl.DeviceIdType.MESH,
        )
        return 0

    lax.fori_loop(1, n, greet, 0)

    q_copy = pltpu.make_async_copy(q_hbm, q_v, local_sem.at[0])
    t_copy = pltpu.make_async_copy(t_hbm, t_v, local_sem.at[1])
    keys_copy = pltpu.make_async_copy(keys_hbm, keys_ref, local_sem.at[3])
    gain_copy = pltpu.make_async_copy(gain_hbm, gain_ref, local_sem.at[4])
    w_copy = pltpu.make_async_copy(w_hbm, w_ref, local_sem.at[5])
    keys_copy.start()
    gain_copy.start()
    w_copy.start()
    q_copy.start()
    t_copy.start()

    keys_copy.wait()
    gain_copy.wait()
    keys3 = keys_ref[...].astype(f32).reshape(nb, STRIDE, DH)
    gain_lo = gain_ref[0:STRIDE, :]
    gain_hi = gain_ref[STRIDE:KERNEL, :]
    low = jnp.sum(keys3 * gain_lo[None], axis=1)
    high = jnp.sum(keys3 * gain_hi[None], axis=1)
    pool_v[me] = (low + jnp.concatenate([high[1:], high[:1]], axis=0)).astype(bf16)
    part_v[me, 0:1] = low[nb - 1 : nb]
    part_v[me, 1:2] = high[0:1]
    part_v[n] = jnp.zeros((8, DH), f32)

    @pl.when(me == n - 1)
    def _():
        halo_v[...] = jnp.zeros((STRIDE, DH), bf16)

    @pl.when(me == 0)
    def _():
        carry_v[...] = jnp.zeros((8, DH), f32)

    pl.semaphore_wait(barrier, n - 1)

    def pool_copy(dst, slot):
        return remote(pool_v.at[slot], pool_v.at[slot], pool_s.at[dst], pool_r.at[slot], dst)

    def part_copy(dst, slot):
        pair = part_v.at[slot, pl.ds(0, 2)]
        return remote(pair, pair, part_s.at[dst], part_r.at[slot], dst)

    def send_pool(k, _):
        dst = lax.rem(me + k, n)
        pool_copy(dst, me).start()
        part_copy(dst, me).start()
        return 0

    lax.fori_loop(1, n, send_pool, 0)

    def halo_copy(dst):
        return remote(
            keys_ref.at[pl.ds(0, STRIDE)], halo_v, side_sem.at[0], side_sem.at[1], dst
        )

    @pl.when(me > 0)
    def _():
        halo_copy(me - 1).start()

    def take_pool(k, _):
        src = lax.rem(me + k, n)
        pool_copy(src, src).wait_recv()
        part_copy(src, src).wait_recv()
        return 0

    lax.fori_loop(1, n, take_pool, 0)
    last_row = lax.broadcasted_iota(jnp.int32, (n, nb, DH), 1) == nb - 1
    edges = part_v[0:n, 0:1, :] + part_v[1 : n + 1, 1:2, :]
    pooled = jnp.where(last_row, edges, pool_v[...].astype(f32)).astype(bf16)
    pooled_v[...] = pooled.reshape(count, DH)
    w_copy.wait()
    comp_v[...] = jnp.dot(
        pooled_v[...], w_ref[...], preferred_element_type=f32
    ).astype(bf16)
    q_copy.wait()
    t_copy.wait()

    place0 = slab_ref[0] * rows
    column_end = STRIDE * lax.broadcasted_iota(jnp.int32, (tr, count), 1) + (KERNEL - 1)
    row_in = lax.broadcasted_iota(jnp.int32, (tr, count), 0)
    nt = (((1,), (1,)), ((), ()))
    tn = (((0,), (0,)), ((), ()))

    def group(base, first, kl):
        rows_at = pl.ds(base, rb)
        for h in range(HEADS):
            qh = q_v[rows_at, h * DH : (h + 1) * DH]
            for c0 in range(0, count, CHUNK):
                s_v[h, :, c0 : c0 + CHUNK] = (
                    lax.dot_general(
                        qh, comp_v[c0 : c0 + CHUNK, :], nt, preferred_element_type=f32
                    )
                    * inv
                )

        def tile(i, kl):
            off = pl.multiple_of(i * tr, tr)
            here = pl.ds(off, tr)
            visible = column_end <= place0 + base + off + row_in
            top_all = jnp.full((tr, count), 2 * big_negative, f32)
            for h in range(HEADS):
                s = jnp.where(visible, s_v[h, here, :], big_negative)
                top = jnp.max(s, axis=1, keepdims=True)
                total = jnp.sum(jnp.exp(s - top), axis=1, keepdims=True)
                lse = jnp.where(top > 0.5 * big_negative, top + jnp.log(total), 0.0)
                x = s - lse
                s_v[h, here, :] = x
                top_all = jnp.maximum(top_all, x)
            mass = jnp.zeros((tr, count), f32)
            for h in range(HEADS):
                u = jnp.exp(s_v[h, here, :] - top_all)
                s_v[h, here, :] = u
                mass = mass + u
            teach = t_v[pl.ds(pl.multiple_of(base + off, tr), tr), :].astype(f32)
            seen = jnp.where(visible, teach, 0.0)
            teach_total = jnp.sum(seen, axis=1, keepdims=True)
            safe = jnp.where(teach_total > 0, teach_total, 1.0)
            tprob = seen / safe
            logm = jnp.where(visible, top_all + jnp.log(mass) - jnp.log(f32(HEADS)), 0.0)
            kl = kl + jnp.sum(
                tprob * (jnp.log(teach) - jnp.log(safe) - logm), axis=1, keepdims=True
            )
            weight = tprob / mass
            peak = jnp.exp(top_all)
            weight_s = loss_scale * weight
            for h in range(HEADS):
                u = s_v[h, here, :]
                cvec = loss_scale * jnp.sum(u * weight, axis=1, keepdims=True)
                g_v[h, here, :] = (u * (peak * cvec - weight_s)).astype(bf16)
            return kl

        kl = lax.fori_loop(0, rb // tr, tile, kl)
        for c0 in range(0, count, CHUNK):
            acc = jnp.zeros((DH, CHUNK), f32)
            for h in range(HEADS):
                acc = acc + lax.dot_general(
                    q_v[rows_at, h * DH : (h + 1) * DH], g_v[h, :, c0 : c0 + CHUNK], tn,
                    preferred_element_type=f32,
                )
            add = acc.T * inv
            for r0 in range(0, CHUNK, nb):
                owner = (c0 + r0) // nb
                at = (owner % 2, owner // 2)
                if first is None:
                    p_v[at] = add[r0 : r0 + nb]
                else:
                    p_v[at] = p_v[at] + add[r0 : r0 + nb]
        return kl

    def query_grads(base):
        for h in range(HEADS):
            gq_ref[pl.ds(base, rb), h * DH : (h + 1) * DH] = (
                jnp.dot(g_v[h], comp_v[...], preferred_element_type=f32) * inv
            ).astype(bf16)

    kl0 = jnp.zeros((tr, 1), f32)
    if rb == rows:
        kl = group(0, None, kl0)
    else:
        p_v[...] = jnp.zeros_like(p_v)

        def step(i, kl):
            base = pl.multiple_of(i * rb, rb)
            kl = group(base, False, kl)
            query_grads(base)
            return kl

        kl = lax.fori_loop(0, rows // rb, step, kl0)

    core = lax.rem(me, 2)
    mine = lax.div(me, 2)
    half = n // 2
    twin = me + 1 - 2 * core

    def pair_copy(slot):
        return remote(
            p_v.at[1 - core, slot], pair_v.at[slot], pair_s.at[slot], pair_r.at[slot], twin
        )

    def rs_copy(dst, slot):
        return remote(
            p_v.at[core, dst], rs_v.at[slot], rs_s.at[dst], rs_r.at[slot], 2 * dst + core
        )

    def send_pair(k, _):
        pair_copy(lax.rem(mine + k, half)).start()
        return 0

    lax.fori_loop(1, half + 1, send_pair, 0)

    def forward(k, _):
        slot = lax.rem(mine + k, half)
        pair_copy(slot).wait_recv()
        p_v[core, slot] = p_v[core, slot] + pair_v[slot]
        rs_copy(slot, mine).start()
        return 0

    lax.fori_loop(1, half, forward, 0)
    pair_copy(mine).wait_recv()
    rs_v[mine] = p_v[core, mine] + pair_v[mine]

    if rb == rows:
        query_grads(0)

    @pl.when(me < n - 1)
    def _():
        halo_copy(me).wait_recv()

    upper3 = jnp.concatenate(
        [keys3[1:], halo_v[...].astype(f32).reshape(1, STRIDE, DH)], axis=0
    )

    def take_rs(k, _):
        slot = lax.rem(mine + k, half)
        rs_copy(slot, slot).wait_recv()
        return 0

    lax.fori_loop(1, half, take_rs, 0)
    own = lax.fori_loop(1, half, lambda d, total: total + rs_v[d], rs_v[0])

    own3 = split3(own)
    gp3 = lax.dot_general(
        jnp.concatenate(own3, axis=0), w_ref[...], nt, preferred_element_type=f32
    )
    grad_pooled = (gp3[2 * nb :] + gp3[nb : 2 * nb]) + gp3[:nb]
    gp_v[...] = grad_pooled

    def carry_copy(dst):
        return remote(
            gp_v.at[pl.ds(nb - 8, 8)], carry_v, side_sem.at[2], side_sem.at[3], dst
        )

    @pl.when(me < n - 1)
    def _():
        carry_copy(me + 1).start()

    pooled_own = pooled_v[pl.ds(pl.multiple_of(me * nb, nb), nb), :]
    comp_part = lax.dot_general(
        jnp.concatenate([pooled_own] * 3, axis=0),
        jnp.concatenate(own3[::-1], axis=0),
        tn,
        preferred_element_type=f32,
    )
    gain_part = jnp.concatenate(
        [
            jnp.sum(grad_pooled[:, None, :] * keys3, axis=0),
            jnp.sum(grad_pooled[:, None, :] * upper3, axis=0),
        ],
        axis=0,
    )
    kl_row = jnp.broadcast_to(jnp.sum(kl, axis=0, keepdims=True), (1, DH))
    slot_rows = a_out.shape[1]
    for d in range(n):
        pieces = [comp_part[d * rc : (d + 1) * rc]]
        if (d + 1) * rg <= KERNEL:
            pieces.append(gain_part[d * rg : (d + 1) * rg])
        else:
            pieces.append(jnp.zeros((rg, DH), f32))
        pieces.append(jnp.broadcast_to(kl_row, (slot_rows - rc - rg, DH)))
        a_out[d] = jnp.concatenate(pieces, axis=0)

    def a_copy(dst, slot):
        used = pl.ds(0, rc + rg + 1)
        return remote(
            a_out.at[dst, used], a_in.at[slot, used], a_s.at[dst], a_r.at[slot], dst
        )

    def send_a(k, _):
        a_copy(lax.rem(me + k, n), me).start()
        return 0

    lax.fori_loop(1, n, send_a, 0)
    a_in[me] = a_out[me]

    @pl.when(me > 0)
    def _():
        carry_copy(me).wait_recv()

    def take_a(k, _):
        a_copy(lax.rem(me + k, n), lax.rem(me + k, n)).wait_recv()
        return 0

    lax.fori_loop(1, n, take_a, 0)
    b_out[...] = lax.fori_loop(1, n, lambda d, total: total + a_in[d], a_in[0])

    def b_copy(dst, slot):
        used = pl.ds(0, rc + rg)
        return remote(
            b_out.at[used], b_in.at[slot, used], b_s.at[dst], b_r.at[slot], dst
        )

    def send_b(k, _):
        b_copy(lax.rem(me + k, n), me).start()
        return 0

    lax.fori_loop(1, n, send_b, 0)
    b_in[me] = b_out[...]
    loss_ref[...] = b_out[rc + rg : rc + rg + 1, :] * (1.0 / (rows * n))

    before = jnp.concatenate([carry_v[7:8, :], grad_pooled[: nb - 1]], axis=0)
    grad_keys = grad_pooled[:, None, :] * gain_lo[None] + before[:, None, :] * gain_hi[None]
    gk_ref[...] = grad_keys.reshape(nb * STRIDE, DH).astype(bf16)

    def drop_sends(k, _):
        dst = lax.rem(me + k, n)
        pool_copy(dst, me).wait_send()
        part_copy(dst, me).wait_send()
        a_copy(dst, me).wait_send()
        return 0

    lax.fori_loop(1, n, drop_sends, 0)

    def drop_pairs(k, _):
        slot = lax.rem(mine + k, half)
        pair_copy(slot).wait_send()
        rs_copy(slot, mine).wait_send()
        return 0

    lax.fori_loop(1, half, drop_pairs, 0)
    pair_copy(mine).wait_send()

    @pl.when(me > 0)
    def _():
        halo_copy(me - 1).wait_send()

    @pl.when(me < n - 1)
    def _():
        carry_copy(me + 1).wait_send()

    def take_b(k, _):
        other = lax.rem(me + k, n)
        b_copy(other, other).wait_recv()
        b_copy(other, me).wait_send()
        return 0

    lax.fori_loop(1, n, take_b, 0)
    for d in range(n):
        gcomp_ref[d * rc : (d + 1) * rc, :] = b_in[d, 0:rc, :]
        if (d + 1) * rg <= KERNEL:
            ggain_ref[d * rg : (d + 1) * rg, :] = b_in[d, rc : rc + rg, :]


def finish(*refs):
    sources, targets, sem = refs[:5], refs[5:10], refs[10]
    copies = [
        pltpu.make_async_copy(source, target, sem.at[i])
        for i, (source, target) in enumerate(zip(sources, targets))
    ]
    for copy in copies:
        copy.start()
    for copy in copies:
        copy.wait()


def body(n, keys, queries, teacher_map, slab_index, pos_gain, w_comp):
    rows, count = teacher_map.shape
    nb = count // n
    rb = rows if count <= 1024 else 32
    tr = min(rb, 64 if count <= 1024 else 16)
    rc = -(-DH // n)
    rg = -(-KERNEL // n)
    slot_rows = -(-(rc + rg + 1) // 8) * 8
    dma = pltpu.SemaphoreType.DMA
    vmem = pl.BlockSpec(memory_space=pltpu.VMEM)
    hbm = pl.BlockSpec(memory_space=pltpu.HBM)
    shapes = (
            jax.ShapeDtypeStruct((1, DH), f32),
            jax.ShapeDtypeStruct((rows, HEADS * DH), bf16),
            jax.ShapeDtypeStruct(keys.shape, bf16),
            jax.ShapeDtypeStruct((DH, DH), f32),
            jax.ShapeDtypeStruct((KERNEL, DH), f32),
        )
    results = pl.pallas_call(
        functools.partial(kernel, n, rb, tr, rc, rg),
        out_shape=shapes,
        in_specs=[pl.BlockSpec(memory_space=pltpu.SMEM)] + [hbm] * 5,
        out_specs=(vmem,) * 5,
        scratch_shapes=[
            pltpu.VMEM(keys.shape, bf16),
            pltpu.VMEM(pos_gain.shape, f32),
            pltpu.VMEM(w_comp.shape, bf16),
            pltpu.VMEM((rows, HEADS * DH), bf16),
            pltpu.VMEM((rows, count), bf16),
            pltpu.VMEM((n, nb, DH), bf16),
            pltpu.VMEM((n + 1, 8, DH), f32),
            pltpu.VMEM((STRIDE, DH), bf16),
            pltpu.VMEM((count, DH), bf16),
            pltpu.VMEM((count, DH), bf16),
            pltpu.VMEM((HEADS, rb, count), f32),
            pltpu.VMEM((HEADS, rb, count), bf16),
            pltpu.VMEM((2, n // 2, nb, DH), f32),
            pltpu.VMEM((n // 2, nb, DH), f32),
            pltpu.VMEM((n // 2, nb, DH), f32),
            pltpu.VMEM((n, slot_rows, DH), f32),
            pltpu.VMEM((n, slot_rows, DH), f32),
            pltpu.VMEM((slot_rows, DH), f32),
            pltpu.VMEM((n, slot_rows, DH), f32),
            pltpu.VMEM((nb, DH), f32),
            pltpu.VMEM((8, DH), f32),
            dma((6,)),
        ]
        + [dma((n,))] * 4
        + [dma((n // 2,))] * 4
        + [dma((n,))] * 4
        + [dma((4,))],
        compiler_params=pltpu.CompilerParams(
            collective_id=0, has_side_effects=True, vmem_limit_bytes=48 * 1024 * 1024
        ),
    )(slab_index, *[pltpu.with_memory_space_constraint(x, pltpu.HBM) for x in (keys, pos_gain, w_comp, queries, teacher_map)])
    any_space = pl.BlockSpec(memory_space=pl.ANY)
    loss, gq, gk, gcomp, ggain = pl.pallas_call(
        finish,
        out_shape=shapes,
        in_specs=[any_space] * 5,
        out_specs=[any_space] * 5,
        scratch_shapes=[dma((5,))],
        compiler_params=pltpu.CompilerParams(vmem_limit_bytes=4 * 1024 * 1024),
    )(*results)
    return (loss[0, 0:1], gq, gk, gcomp, ggain)


def solution(mesh):
    in_specs = (
        P(("groups", "ctx"), None),
        P(("groups", "ctx"), None),
        P(("groups", "ctx"), None),
        P(("groups", "ctx")),
        P(),
        P(),
    )
    out_specs = (
        P("groups"),
        P(("groups", "ctx"), None),
        P(("groups", "ctx"), None),
        P("groups", None),
        P("groups", None),
    )
    return jax.shard_map(
        functools.partial(body, mesh.shape["ctx"]),
        mesh=mesh, in_specs=in_specs, out_specs=out_specs, check_vma=False,
    )
```
